128 devices in a mesh: gx: 8 (over y, core), gy: 4 (over z), gz: 4 (over x).
Axes of the slice: x: 4, y: 4, z: 4, core: 2. Of those that a mesh axis runs over, the one named last changes fastest.
Arguments:
- source_field: bfloat16 [2, 2, 16, 512, 2048], P(None, None, 'gz', 'gy', 'gx'), may hold values from -6 to 6
- adjoint_source: bfloat16 [2, 2, 16, 512, 2048], P(None, None, 'gz', 'gy', 'gx'), may hold values from -6 to 6
- x_inverse: bfloat16 [8, 4, 2, 256, 256], P('gx', 'gy'), may hold values from -1 to 1.25
- y_inverse: bfloat16 [8, 4, 2, 128, 128], P('gx', 'gy'), may hold values from -1 to 1.25
Outputs:
- state_field: bfloat16 [2, 2, 16, 512, 2048], P(None, None, 'gz', 'gy', 'gx')
- adjoint_field: bfloat16 [2, 2, 16, 512, 2048], P(None, None, 'gz', 'gy', 'gx')
- gradient: float32 [16, 512, 2048], P('gz', 'gy', 'gx')
The draws below stay inside these ranges and needn't reach their ends.
All inputs are finite; a program needn't handle non-finite values.
Results may differ from the reference program's by a relative error of at most 0.017.
Values may be sent and summed in bfloat16 or wider, within the bound.
A program may use at most 64 MiB of HBM per device.

```python
import math
import jax
import jax.numpy as jnp

LINE_X = 256
LINE_Y = 128
SHOTS = 2
SUB_X = 8
SUB_Y = 4
GRID_X = 2048
GRID_Y = 512
GRID_Z = 16
N_GX = 8
N_GY = 4


def inverse_draw(key, matrix_order):
    key_list = jax.random.split(key, 4)
    full_shape = (SUB_X, SUB_Y, 2, matrix_order, matrix_order)
    spread = 0.6 / math.sqrt(matrix_order)
    noise_part = jnp.clip(jax.random.normal(key_list[0], full_shape, jnp.float32), -3.0, 3.0) * spread
    diag_real = jax.random.uniform(key_list[1], (SUB_X, SUB_Y, matrix_order), jnp.float32, 0.7, 1.1)
    diag_imag = jax.random.uniform(key_list[2], (SUB_X, SUB_Y, matrix_order), jnp.float32, -0.3, 0.3)
    phase_angle = jax.random.uniform(key_list[3], (SUB_X, SUB_Y), jnp.float32, -math.pi, math.pi)
    row_ids = jnp.arange(matrix_order)[:, None]
    col_ids = jnp.arange(matrix_order)[None, :]
    identity = (row_ids == col_ids).astype(jnp.float32)
    corner_mask = ((row_ids == matrix_order - 1) & (col_ids == 0)).astype(jnp.float32)
    off_diagonal = noise_part * (1.0 - identity - corner_mask)
    diagonal = jnp.stack([diag_real, diag_imag], axis=2)[..., None] * identity
    transmit = jnp.stack([0.9 * jnp.cos(phase_angle), 0.9 * jnp.sin(phase_angle)], axis=2)[..., None, None] * corner_mask
    return (off_diagonal + diagonal + transmit).astype(jnp.bfloat16)


def draw_x_inverse(key, part):
    return inverse_draw(jax.random.fold_in(key, 11), LINE_X)


def draw_y_inverse(key, part):
    return inverse_draw(jax.random.fold_in(key, 23), LINE_Y)


def steps_of(rng, shape, cuts, least, high):
    gain, own = 1.0, jax.random.fold_in(rng, 6)
    for position, blocks in cuts:
        draws = jnp.exp(jax.random.uniform(jax.random.fold_in(own, position), (blocks,), jnp.float32, least / len(cuts), high / len(cuts)))
        gain = gain * jnp.repeat(draws, shape[position] // blocks).reshape([-1 if axis == position else 1 for axis in range(len(shape))])
    return gain


def gaussian(key, dims, deviation, reach, shards=(), kind=jnp.bfloat16):
    entries = deviation * jax.random.normal(key, dims, jnp.float32)
    if shards:
        entries = entries * steps_of(key, dims, shards, -0.22, 0.18)
    return jnp.clip(entries, -reach, reach).astype(kind)


def setup_inputs(seed: int = 0) -> dict:
    streams_of = jax.random.split(jax.random.key(seed), 5)
    return {
        "source_field": gaussian(streams_of[0], (SHOTS, 2, GRID_Z, GRID_Y, GRID_X), 1.0, 6.0, ((2, 4), (3, 4), (4, 8))),
        "adjoint_source": gaussian(streams_of[1], (SHOTS, 2, GRID_Z, GRID_Y, GRID_X), 1.0, 6.0, ((2, 4), (3, 4), (4, 8))),
        "x_inverse": draw_x_inverse(jax.random.fold_in(streams_of[4], 71), 0),
        "y_inverse": draw_y_inverse(jax.random.fold_in(streams_of[4], 71), 0),
    }


def combine_parts(real_term, imag_term):
    real_out = real_term[:, 0] - imag_term[:, 1]
    imag_out = imag_term[:, 0] + real_term[:, 1]
    return jnp.stack([real_out, imag_out], axis=1).astype(jnp.bfloat16)


def solve_along_x(field, real_matrix, imag_matrix, form):
    wide = field.astype(jnp.float32)
    real_term = jnp.einsum(form, wide, real_matrix.astype(jnp.float32))
    imag_term = jnp.einsum(form, wide, imag_matrix.astype(jnp.float32))
    return combine_parts(real_term, imag_term)


def solve_along_y(field, real_matrix, imag_matrix, form):
    wide = field.astype(jnp.float32)
    real_term = jnp.einsum(form, real_matrix.astype(jnp.float32), wide)
    imag_term = jnp.einsum(form, imag_matrix.astype(jnp.float32), wide)
    return combine_parts(real_term, imag_term)


def depth_average(field):
    padded = jnp.pad(field.astype(jnp.float32), ((0, 0), (0, 0), (1, 1), (0, 0), (0, 0)))
    return (0.5 * padded[:, :, 1:-1] + 0.25 * (padded[:, :, :-2] + padded[:, :, 2:])).astype(jnp.bfloat16)


def reference(source_field, adjoint_source, x_inverse, y_inverse):
    def block_of(field, row_index, column_index):
        return field[:, :, :, column_index * LINE_Y:(column_index + 1) * LINE_Y, row_index * LINE_X:(row_index + 1) * LINE_X]

    def assemble(blocks):
        columns_list = []
        for row_index in range(N_GX):
            pieces = [blocks[(row_index, column_index)] for column_index in range(N_GY)]
            columns_list.append(jnp.concatenate(pieces, axis=3))
        return jnp.concatenate(columns_list, axis=4)

    state_blocks = {}
    for row_index in range(N_GX):
        for column_index in range(N_GY):
            x_pair = x_inverse[row_index, column_index]
            y_pair = y_inverse[row_index, column_index]
            rhs_value = block_of(source_field, row_index, column_index).astype(jnp.float32)
            if row_index > 0:
                rhs_value = rhs_value.at[..., 0].add(state_blocks[(row_index - 1, column_index)][..., LINE_X - 1].astype(jnp.float32))
            if column_index > 0:
                rhs_value = rhs_value.at[:, :, :, 0, :].add(state_blocks[(row_index, column_index - 1)][:, :, :, LINE_Y - 1, :].astype(jnp.float32))
            half_value = solve_along_x(rhs_value.astype(jnp.bfloat16), x_pair[0], x_pair[1], "bcdyx,wx->bcdyw")
            state_blocks[(row_index, column_index)] = solve_along_y(half_value, y_pair[0], y_pair[1], "py,bcdyx->bcdpx")

    adjoint_blocks = {}
    for row_index in reversed(range(N_GX)):
        for column_index in reversed(range(N_GY)):
            x_pair = x_inverse[row_index, column_index]
            y_pair = y_inverse[row_index, column_index]
            rhs_value = block_of(adjoint_source, row_index, column_index).astype(jnp.float32)
            if row_index < N_GX - 1:
                rhs_value = rhs_value.at[..., LINE_X - 1].add(adjoint_blocks[(row_index + 1, column_index)][..., 0].astype(jnp.float32))
            if column_index < N_GY - 1:
                rhs_value = rhs_value.at[:, :, :, LINE_Y - 1, :].add(adjoint_blocks[(row_index, column_index + 1)][:, :, :, 0, :].astype(jnp.float32))
            half_value = solve_along_x(rhs_value.astype(jnp.bfloat16), x_pair[0], x_pair[1], "bcdyx,xw->bcdyw")
            adjoint_blocks[(row_index, column_index)] = solve_along_y(half_value, y_pair[0], y_pair[1], "yp,bcdyx->bcdpx")

    state_out = depth_average(assemble(state_blocks))
    adjoint_out = depth_average(assemble(adjoint_blocks))
    state_wide = state_out.astype(jnp.float32)
    adjoint_wide = adjoint_out.astype(jnp.float32)
    product = state_wide[:, 0] * adjoint_wide[:, 0] - state_wide[:, 1] * adjoint_wide[:, 1]
    gradient = jnp.sum(product, axis=0) / SHOTS
    return state_out, adjoint_out, gradient
```

```python
import functools

import jax
import jax.numpy as jnp
from jax import lax
from jax.experimental import pallas as pl
from jax.experimental.pallas import tpu as pltpu
from jax.sharding import PartitionSpec as P

MESH = pl.DeviceIdType.MESH
BF = jnp.bfloat16
F32 = jnp.float32


def dot(left, right):
    return jnp.dot(left, right, preferred_element_type=F32)


def dot_last(left, right):
    return lax.dot_general(left, right, (((1,), (1,)), ((), ())), preferred_element_type=F32)


def dot_first(left, right):
    return lax.dot_general(left, right, (((0,), (0,)), ((), ())), preferred_element_type=F32)


def kernel(
    sizes, shots, depths, ny, nx,
    s_hbm, a_hbm, x_hbm, y_hbm, so_hbm, ao_hbm, g_hbm,
    src, xraw, yraw, xmat, gmat, ymat, edge, sxv, ysv, ext, ab, plane_out, plane_in,
    c_in, r_in, c_out, r_out, pq, half, base, field, grad,
    load_sem, plane_send, plane_recv, halo_send, halo_recv,
    c_send, c_recv, r_send, r_recv, out_sem, grad_sem,
):
    n_gx, n_gy, n_gz = sizes
    gx, gy, gz = lax.axis_index("gx"), lax.axis_index("gy"), lax.axis_index("gz")
    rhs = shots * depths
    c_in[...] = jnp.zeros_like(c_in)
    r_in[...] = jnp.zeros_like(r_in)
    barrier = pltpu.get_barrier_semaphore()
    for axis, index, count in (("gx", gx, n_gx), ("gy", gy, n_gy), ("gz", gz, n_gz)):
        @pl.when(index > 0)
        def _():
            pl.semaphore_signal(barrier, inc=1, device_id={axis: index - 1}, device_id_type=MESH)

        @pl.when(index < count - 1)
        def _():
            pl.semaphore_signal(barrier, inc=1, device_id={axis: index + 1}, device_id_type=MESH)

    loads = [
        pltpu.make_async_copy(x_hbm.at[0, 0], xraw, load_sem.at[0]),
        pltpu.make_async_copy(y_hbm.at[0, 0], yraw, load_sem.at[1]),
        pltpu.make_async_copy(s_hbm, src.at[0, :, :, pl.ds(1, depths)], load_sem.at[2]),
        pltpu.make_async_copy(a_hbm, src.at[1, :, :, pl.ds(1, depths)], load_sem.at[3]),
    ]
    for load in loads:
        load.start()

    @pl.when(gz == 0)
    def _():
        plane_in[:, 0] = jnp.zeros_like(plane_in[:, 0])
        src[:, :, :, 0] = jnp.zeros_like(src[:, :, :, 0])

    @pl.when(gz == n_gz - 1)
    def _():
        plane_in[:, 1] = jnp.zeros_like(plane_in[:, 1])
        src[:, :, :, depths + 1] = jnp.zeros_like(src[:, :, :, depths + 1])

    loads[0].wait()
    loads[1].wait()
    for way in range(2):
        xr, xi, yr, yi = xraw[0], xraw[1], yraw[0], yraw[1]
        xrt, xit, yrt, yit = xr.T, xi.T, yr.T, yi.T
        mr, mi = (xrt, xit) if way == 0 else (xr, xi)
        gr, gi = (yrt, yit) if way == 0 else (yr, yi)
        lr, li = (yr, yi) if way == 0 else (yrt, yit)
        xmat[way, :nx, :nx] = mr
        xmat[way, :nx, nx:] = mi
        xmat[way, nx:, :nx] = -mi
        xmat[way, nx:, nx:] = mr
        gmat[way, :ny, :ny] = gr
        gmat[way, :ny, ny:] = gi
        gmat[way, ny:, :ny] = -gi
        gmat[way, ny:, ny:] = gr
        ymat[way, :ny, :ny] = lr
        ymat[way, :ny, ny:] = -li
        ymat[way, ny:, :ny] = li
        ymat[way, ny:, ny:] = lr
        x_row = 0 if way == 0 else nx - 1
        y_row = 0 if way == 0 else ny - 1
        xe = jnp.concatenate([mr[x_row:x_row + 1], mi[x_row:x_row + 1]], axis=1).astype(F32)
        ye = jnp.concatenate([gr[y_row:y_row + 1], gi[y_row:y_row + 1]], axis=1).astype(F32)
        edge[way, 0:1, : 2 * ny] = ye
        edge[way, 0:1, 2 * ny:] = xe

    loads[2].wait()
    loads[3].wait()

    def pair_rows(real, imag):
        rows = lax.broadcasted_iota(jnp.int32, (8, 1), 0)
        first = jnp.where(rows == 0, real, jnp.where(rows == 1, imag, 0.0))
        second = jnp.where(rows == 0, -imag, jnp.where(rows == 1, real, 0.0))
        return first.astype(BF), second.astype(BF)

    def plane_copies(way):
        down = pltpu.make_async_remote_copy(
            src_ref=plane_out.at[way, 0], dst_ref=plane_in.at[way, 1],
            send_sem=plane_send.at[way, 0], recv_sem=plane_recv.at[way, 1],
            device_id={"gz": gz - 1}, device_id_type=MESH,
        )
        up = pltpu.make_async_remote_copy(
            src_ref=plane_out.at[way, 1], dst_ref=plane_in.at[way, 0],
            send_sem=plane_send.at[way, 1], recv_sem=plane_recv.at[way, 0],
            device_id={"gz": gz + 1}, device_id_type=MESH,
        )
        return down, up

    def halo_copies(way):
        down = pltpu.make_async_remote_copy(
            src_ref=src.at[way, :, :, 1], dst_ref=src.at[way, :, :, depths + 1],
            send_sem=halo_send.at[way, 0], recv_sem=halo_recv.at[way, 1],
            device_id={"gz": gz - 1}, device_id_type=MESH,
        )
        up = pltpu.make_async_remote_copy(
            src_ref=src.at[way, :, :, depths], dst_ref=src.at[way, :, :, 0],
            send_sem=halo_send.at[way, 1], recv_sem=halo_recv.at[way, 0],
            device_id={"gz": gz + 1}, device_id_type=MESH,
        )
        return down, up

    def start_both(copies):
        @pl.when(gz > 0)
        def _():
            copies[0].start()

        @pl.when(gz < n_gz - 1)
        def _():
            copies[1].start()

    def wait_arrivals(copies):
        @pl.when(gz > 0)
        def _():
            copies[1].wait_recv()

        @pl.when(gz < n_gz - 1)
        def _():
            copies[0].wait_recv()

    def wait_departures(copies):
        @pl.when(gz > 0)
        def _():
            copies[0].wait_send()

        @pl.when(gz < n_gz - 1)
        def _():
            copies[1].wait_send()

    def local_terms(way):
        other = edge[1 - way, 0:1, :]
        x_first, x_second = pair_rows(other[:, 2 * ny: 2 * ny + nx], other[:, 2 * ny + nx:])
        y_first, y_second = pair_rows(other[:, :ny], other[:, ny: 2 * ny])
        y_both = jnp.concatenate([y_first, y_second], axis=1)
        for s in range(shots):
            for d in range(0, depths, 2):
                real = src[way, s, 0, pl.ds(1 + d, 2)].reshape(2 * ny, nx)
                imag = src[way, s, 1, pl.ds(1 + d, 2)].reshape(2 * ny, nx)
                res = dot_last(x_first, real) + dot_last(x_second, imag)
                for k in range(2):
                    q = (d + k) * shots + s
                    sxv[q:q + 1, :ny] = res[0:1, k * ny:(k + 1) * ny]
                    sxv[q:q + 1, ny:] = res[1:2, k * ny:(k + 1) * ny]
            for d in range(depths):
                both = jnp.concatenate([src[way, s, 0, 1 + d], src[way, s, 1, 1 + d]], axis=0)
                res = dot(y_both, both)
                q = d * shots + s
                ysv[q:q + 1, :nx] = res[0:1]
                ysv[q:q + 1, nx:] = res[1:2]
        col = dot(sxv[...].astype(BF), gmat[way])
        row = dot(ysv[...].astype(BF), xmat[way])
        ab[way, :, : 2 * ny] = col
        ab[way, :, 2 * ny:] = row
        plane_out[way, 0] = ab[way, :shots]
        plane_out[way, 1] = ab[way, rhs - shots:]

    def averaged_terms(way):
        ext[:shots] = plane_in[way, 0]
        ext[shots:shots + rhs] = ab[way]
        ext[shots + rhs:rhs + 2 * shots] = plane_in[way, 1]
        near = ext[:rhs] + ext[2 * shots: 2 * shots + rhs]
        ab[way] = 0.5 * ext[shots:shots + rhs] + 0.25 * near

    def hop_copies(way):
        step = 1 - 2 * way
        col = pltpu.make_async_remote_copy(
            src_ref=c_out.at[way], dst_ref=c_in.at[way],
            send_sem=c_send.at[way], recv_sem=c_recv.at[way],
            device_id={"gx": gx + step}, device_id_type=MESH,
        )
        row = pltpu.make_async_remote_copy(
            src_ref=r_out.at[way], dst_ref=r_in.at[way],
            send_sem=r_send.at[way], recv_sem=r_recv.at[way],
            device_id={"gy": gy + step}, device_id_type=MESH,
        )
        return col, row

    def places(way):
        at_x = gx + way * (n_gx - 1 - 2 * gx)
        at_y = gy + way * (n_gy - 1 - 2 * gy)
        return at_x, at_y

    def hop(way):
        at_x, at_y = places(way)
        send_col, send_row = hop_copies(way)

        @pl.when(at_x > 0)
        def _():
            send_col.wait_recv()

        @pl.when(at_y > 0)
        def _():
            send_row.wait_recv()

        p = dot(c_in[way], gmat[way])
        q = dot(r_in[way], xmat[way])
        pq[way, :, : 2 * ny] = p
        pq[way, :, 2 * ny:] = q
        forward = jnp.broadcast_to(way == 0, (1, 1))

        def out_lane(value):
            n = value.shape[1]
            return jnp.where(forward, value[:, n - 1:], value[:, :1])

        ey, ex = edge[way, 0:1, : 2 * ny], edge[way, 0:1, 2 * ny:]
        eyr, eyi, exr, exi = ey[:, :ny], ey[:, ny:], ex[:, :nx], ex[:, nx:]
        pr, pi, qr, qi = p[:, :ny], p[:, ny:], q[:, :nx], q[:, nx:]
        xr, xi, yr, yi = out_lane(exr), out_lane(exi), out_lane(eyr), out_lane(eyi)
        tr, ti, sr, si = out_lane(pr), out_lane(pi), out_lane(qr), out_lane(qi)
        c_out[way, :, :ny] = (ab[way, :, :ny] + (pr * xr - pi * xi) + (eyr * sr - eyi * si)).astype(BF)
        c_out[way, :, ny:] = (
            ab[way, :, ny: 2 * ny] + (pr * xi + pi * xr) + (eyr * si + eyi * sr)
        ).astype(BF)

        @pl.when(at_x < n_gx - 1)
        def _():
            send_col.start()

        r_out[way, :, :nx] = (
            ab[way, :, 2 * ny: 2 * ny + nx] + (exr * tr - exi * ti) + (qr * yr - qi * yi)
        ).astype(BF)
        r_out[way, :, nx:] = (
            ab[way, :, 2 * ny + nx:] + (exr * ti + exi * tr) + (qr * yi + qi * yr)
        ).astype(BF)

        @pl.when(at_y < n_gy - 1)
        def _():
            send_row.start()

    def hop_departures(way):
        at_x, at_y = places(way)
        send_col, send_row = hop_copies(way)

        @pl.when(at_x < n_gx - 1)
        def _():
            send_col.wait_send()

        @pl.when(at_y < n_gy - 1)
        def _():
            send_row.wait_send()

    def base_fields(way):
        def two_depths(i, carry):
            s, d = i // (depths // 2), (i % (depths // 2)) * 2
            planes = []
            for part in range(2):
                low = src[way, s, part, pl.ds(d, 2)].astype(F32)
                mid = src[way, s, part, pl.ds(d + 1, 2)].astype(F32)
                high = src[way, s, part, pl.ds(d + 2, 2)].astype(F32)
                mean = 0.5 * mid + 0.25 * (low + high)
                planes.append(mean.astype(BF).reshape(2 * ny, nx))
            out = dot(jnp.concatenate(planes, axis=1), xmat[way])
            for k in range(2):
                half[k, :ny] = out[k * ny:(k + 1) * ny, :nx].astype(BF)
                half[k, ny:] = out[k * ny:(k + 1) * ny, nx:].astype(BF)
            for k in range(2):
                base[way, (d + k) * shots + s] = dot(ymat[way], half[k])
            return carry

        lax.fori_loop(0, shots * depths // 2, two_depths, 0)

    def out_copies(way, d):
        target = so_hbm if way == 0 else ao_hbm
        return pltpu.make_async_copy(field.at[way, :, :, d], target.at[:, :, d], out_sem.at[way, d])

    def grad_copy(d):
        return pltpu.make_async_copy(grad.at[d], g_hbm.at[d], grad_sem.at[d])

    def final_fields(way, with_gradient):
        ey, ex = edge[way, 0:1, : 2 * ny], edge[way, 0:1, 2 * ny:]
        ey_turned = jnp.concatenate([-ey[:, ny:], ey[:, :ny]], axis=1)
        ones = lax.broadcasted_iota(jnp.int32, (8, 1), 0)

        def one_depth(d, carry):
            for s in range(shots):
                now = pq[way, pl.ds(d * shots + s, 1), :]
                p, q = now[:, : 2 * ny], now[:, 2 * ny:]
                turned = jnp.concatenate([-p[:, ny:], p[:, :ny]], axis=1)
                left = jnp.where(
                    ones == 0, p,
                    jnp.where(ones == 1, turned, jnp.where(ones == 2, ey, jnp.where(ones == 3, ey_turned, 0.0))),
                ).astype(BF)
                right = jnp.where(
                    ones == 0, ex[:, :nx],
                    jnp.where(
                        ones == 1, ex[:, nx:],
                        jnp.where(ones == 2, q[:, :nx], jnp.where(ones == 3, q[:, nx:], 0.0)),
                    ),
                ).astype(BF)
                total = (base[way, d * shots + s] + dot_first(left, right)).astype(BF)
                field[way, s, 0, d] = total[:ny]
                field[way, s, 1, d] = total[ny:]
            for side in range(2):
                @pl.when(way == side)
                def _():
                    out_copies(side, d).start()
            if with_gradient:
                acc = jnp.zeros((ny, nx), F32)
                for s in range(shots):
                    acc = acc + field[0, s, 0, d].astype(F32) * field[1, s, 0, d].astype(F32)
                    acc = acc - field[0, s, 1, d].astype(F32) * field[1, s, 1, d].astype(F32)
                grad[d] = acc / shots
                grad_copy(d).start()
            return carry

        lax.fori_loop(0, depths, one_depth, 0)

    state_front = gx + gy
    last_front = n_gx + n_gy - 2
    first = jnp.where(2 * state_front <= last_front, 0, 1)
    second = 1 - first
    early = jnp.minimum(state_front, last_front - state_front)

    local_terms(first)
    pl.semaphore_wait(
        barrier,
        sum(
            (index > 0).astype(jnp.int32) + (index < count - 1).astype(jnp.int32)
            for index, count in ((gx, n_gx), (gy, n_gy), (gz, n_gz))
        ),
    )
    start_both(plane_copies(first))
    local_terms(second)
    start_both(plane_copies(second))
    start_both(halo_copies(first))
    start_both(halo_copies(second))
    wait_arrivals(plane_copies(first))
    averaged_terms(first)
    hop(first)
    wait_arrivals(plane_copies(second))
    averaged_terms(second)

    near_middle = early >= 3

    @pl.when(near_middle)
    def _():
        hop(second)

    wait_arrivals(halo_copies(first))
    base_fields(first)
    final_fields(first, False)
    wait_arrivals(halo_copies(second))
    base_fields(second)

    @pl.when(jnp.logical_not(near_middle))
    def _():
        hop(second)

    final_fields(second, True)
    for way in range(2):
        wait_departures(plane_copies(way))
        wait_departures(halo_copies(way))
        hop_departures(way)
        for d in range(depths):
            out_copies(way, d).wait()
    for d in range(depths):
        grad_copy(d).wait()


def per_device(source_field, adjoint_source, x_inverse, y_inverse):
    shots, _, depths, ny, nx = source_field.shape
    sizes = tuple(lax.axis_size(axis) for axis in ("gx", "gy", "gz"))
    rhs = shots * depths
    wide = 2 * (ny + nx)
    vmem = pltpu.VMEM
    dma = pltpu.SemaphoreType.DMA
    anywhere = pl.BlockSpec(memory_space=pl.ANY)
    return pl.pallas_call(
        functools.partial(kernel, sizes, shots, depths, ny, nx),
        out_shape=(
            jax.ShapeDtypeStruct(source_field.shape, BF),
            jax.ShapeDtypeStruct(source_field.shape, BF),
            jax.ShapeDtypeStruct((depths, ny, nx), F32),
        ),
        in_specs=[anywhere] * 4,
        out_specs=(anywhere,) * 3,
        scratch_shapes=[
            vmem((2, shots, 2, depths + 2, ny, nx), BF),
            vmem((2, nx, nx), BF),
            vmem((2, ny, ny), BF),
            vmem((2, 2 * nx, 2 * nx), BF),
            vmem((2, 2 * ny, 2 * ny), BF),
            vmem((2, 2 * ny, 2 * ny), BF),
            vmem((2, 8, wide), F32),
            vmem((rhs, 2 * ny), F32),
            vmem((rhs, 2 * nx), F32),
            vmem((rhs + 2 * shots, wide), F32),
            vmem((2, rhs, wide), F32),
            vmem((2, 2, shots, wide), F32),
            vmem((2, 2, shots, wide), F32),
            vmem((2, rhs, 2 * ny), BF),
            vmem((2, rhs, 2 * nx), BF),
            vmem((2, rhs, 2 * ny), BF),
            vmem((2, rhs, 2 * nx), BF),
            vmem((2, rhs, wide), F32),
            vmem((2, 2 * ny, nx), BF),
            vmem((2, rhs, 2 * ny, nx), F32),
            vmem((2, shots, 2, depths, ny, nx), BF),
            vmem((depths, ny, nx), F32),
            dma((4,)),
            dma((2, 2)),
            dma((2, 2)),
            dma((2, 2)),
            dma((2, 2)),
            dma((2,)),
            dma((2,)),
            dma((2,)),
            dma((2,)),
            dma((2, depths)),
            dma((depths,)),
        ],
        compiler_params=pltpu.CompilerParams(collective_id=0, has_side_effects=True),
    )(source_field, adjoint_source, x_inverse, y_inverse)


def solution(mesh):
    in_specs = (
        P(None, None, "gz", "gy", "gx"),
        P(None, None, "gz", "gy", "gx"),
        P("gx", "gy", None, None, None),
        P("gx", "gy", None, None, None),
    )
    out_specs = (
        P(None, None, "gz", "gy", "gx"),
        P(None, None, "gz", "gy", "gx"),
        P("gz", "gy", "gx"),
    )
    return jax.shard_map(
        per_device, mesh=mesh, in_specs=in_specs, out_specs=out_specs, check_vma=False
    )
```

```python
import functools

import jax
import jax.numpy as jnp
from jax import lax
from jax.experimental import pallas as pl
from jax.experimental.pallas import tpu as pltpu
from jax.sharding import PartitionSpec as P

MESH = pl.DeviceIdType.MESH
BF = jnp.bfloat16
F32 = jnp.float32
LIMIT = 24 * 1024 * 1024


def dot(left, right):
    return jnp.dot(left, right, preferred_element_type=F32)


def dot_last(left, right):
    return lax.dot_general(left, right, (((1,), (1,)), ((), ())), preferred_element_type=F32)


def dot_first(left, right):
    return lax.dot_general(left, right, (((0,), (0,)), ((), ())), preferred_element_type=F32)


def kernel(
    sizes, shots, depths, ny, nx,
    s_hbm, a_hbm, x_hbm, y_hbm, base, pq, edge,
    src, xraw, yraw, xmat, gmat, ymat, sxv, ysv, ext, ab, plane_out, plane_in,
    c_in, r_in, c_out, r_out, half,
    load_sem, plane_send, plane_recv, halo_send, halo_recv,
    c_send, c_recv, r_send, r_recv,
):
    n_gx, n_gy, n_gz = sizes
    gx, gy, gz = lax.axis_index("gx"), lax.axis_index("gy"), lax.axis_index("gz")
    rhs = shots * depths
    c_in[...] = jnp.zeros_like(c_in)
    r_in[...] = jnp.zeros_like(r_in)
    barrier = pltpu.get_barrier_semaphore()
    for axis, index, count in (("gx", gx, n_gx), ("gy", gy, n_gy), ("gz", gz, n_gz)):
        @pl.when(index > 0)
        def _():
            pl.semaphore_signal(barrier, inc=1, device_id={axis: index - 1}, device_id_type=MESH)

        @pl.when(index < count - 1)
        def _():
            pl.semaphore_signal(barrier, inc=1, device_id={axis: index + 1}, device_id_type=MESH)

    loads = [
        pltpu.make_async_copy(x_hbm.at[0, 0], xraw, load_sem.at[0]),
        pltpu.make_async_copy(y_hbm.at[0, 0], yraw, load_sem.at[1]),
        pltpu.make_async_copy(s_hbm, src.at[0, :, :, pl.ds(1, depths)], load_sem.at[2]),
        pltpu.make_async_copy(a_hbm, src.at[1, :, :, pl.ds(1, depths)], load_sem.at[3]),
    ]
    for load in loads:
        load.start()

    @pl.when(gz == 0)
    def _():
        plane_in[:, 0] = jnp.zeros_like(plane_in[:, 0])
        src[:, :, :, 0] = jnp.zeros_like(src[:, :, :, 0])

    @pl.when(gz == n_gz - 1)
    def _():
        plane_in[:, 1] = jnp.zeros_like(plane_in[:, 1])
        src[:, :, :, depths + 1] = jnp.zeros_like(src[:, :, :, depths + 1])

    loads[0].wait()
    loads[1].wait()
    for way in range(2):
        xr, xi, yr, yi = xraw[0], xraw[1], yraw[0], yraw[1]
        xrt, xit, yrt, yit = xr.T, xi.T, yr.T, yi.T
        mr, mi = (xrt, xit) if way == 0 else (xr, xi)
        gr, gi = (yrt, yit) if way == 0 else (yr, yi)
        lr, li = (yr, yi) if way == 0 else (yrt, yit)
        xmat[way, :nx, :nx] = mr
        xmat[way, :nx, nx:] = mi
        xmat[way, nx:, :nx] = -mi
        xmat[way, nx:, nx:] = mr
        gmat[way, :ny, :ny] = gr
        gmat[way, :ny, ny:] = gi
        gmat[way, ny:, :ny] = -gi
        gmat[way, ny:, ny:] = gr
        ymat[way, :ny, :ny] = lr
        ymat[way, :ny, ny:] = -li
        ymat[way, ny:, :ny] = li
        ymat[way, ny:, ny:] = lr
        x_row = 0 if way == 0 else nx - 1
        y_row = 0 if way == 0 else ny - 1
        xe = jnp.concatenate([mr[x_row:x_row + 1], mi[x_row:x_row + 1]], axis=1).astype(F32)
        ye = jnp.concatenate([gr[y_row:y_row + 1], gi[y_row:y_row + 1]], axis=1).astype(F32)
        edge[way, 0:1, : 2 * ny] = ye
        edge[way, 0:1, 2 * ny:] = xe

    loads[2].wait()
    loads[3].wait()

    def pair_rows(real, imag):
        rows = lax.broadcasted_iota(jnp.int32, (8, 1), 0)
        first = jnp.where(rows == 0, real, jnp.where(rows == 1, imag, 0.0))
        second = jnp.where(rows == 0, -imag, jnp.where(rows == 1, real, 0.0))
        return first.astype(BF), second.astype(BF)

    def plane_copies(way):
        down = pltpu.make_async_remote_copy(
            src_ref=plane_out.at[way, 0], dst_ref=plane_in.at[way, 1],
            send_sem=plane_send.at[way, 0], recv_sem=plane_recv.at[way, 1],
            device_id={"gz": gz - 1}, device_id_type=MESH,
        )
        up = pltpu.make_async_remote_copy(
            src_ref=plane_out.at[way, 1], dst_ref=plane_in.at[way, 0],
            send_sem=plane_send.at[way, 1], recv_sem=plane_recv.at[way, 0],
            device_id={"gz": gz + 1}, device_id_type=MESH,
        )
        return down, up

    def halo_copies(way):
        down = pltpu.make_async_remote_copy(
            src_ref=src.at[way, :, :, 1], dst_ref=src.at[way, :, :, depths + 1],
            send_sem=halo_send.at[way, 0], recv_sem=halo_recv.at[way, 1],
            device_id={"gz": gz - 1}, device_id_type=MESH,
        )
        up = pltpu.make_async_remote_copy(
            src_ref=src.at[way, :, :, depths], dst_ref=src.at[way, :, :, 0],
            send_sem=halo_send.at[way, 1], recv_sem=halo_recv.at[way, 0],
            device_id={"gz": gz + 1}, device_id_type=MESH,
        )
        return down, up

    def start_both(copies):
        @pl.when(gz > 0)
        def _():
            copies[0].start()

        @pl.when(gz < n_gz - 1)
        def _():
            copies[1].start()

    def wait_arrivals(copies):
        @pl.when(gz > 0)
        def _():
            copies[1].wait_recv()

        @pl.when(gz < n_gz - 1)
        def _():
            copies[0].wait_recv()

    def wait_departures(copies):
        @pl.when(gz > 0)
        def _():
            copies[0].wait_send()

        @pl.when(gz < n_gz - 1)
        def _():
            copies[1].wait_send()

    def local_terms(way):
        other = edge[1 - way, 0:1, :]
        x_first, x_second = pair_rows(other[:, 2 * ny: 2 * ny + nx], other[:, 2 * ny + nx:])
        y_first, y_second = pair_rows(other[:, :ny], other[:, ny: 2 * ny])
        y_both = jnp.concatenate([y_first, y_second], axis=1)
        for s in range(shots):
            for d in range(0, depths, 2):
                real = src[way, s, 0, pl.ds(1 + d, 2)].reshape(2 * ny, nx)
                imag = src[way, s, 1, pl.ds(1 + d, 2)].reshape(2 * ny, nx)
                res = dot_last(x_first, real) + dot_last(x_second, imag)
                for k in range(2):
                    q = (d + k) * shots + s
                    sxv[q:q + 1, :ny] = res[0:1, k * ny:(k + 1) * ny]
                    sxv[q:q + 1, ny:] = res[1:2, k * ny:(k + 1) * ny]
            for d in range(depths):
                both = jnp.concatenate([src[way, s, 0, 1 + d], src[way, s, 1, 1 + d]], axis=0)
                res = dot(y_both, both)
                q = d * shots + s
                ysv[q:q + 1, :nx] = res[0:1]
                ysv[q:q + 1, nx:] = res[1:2]
        col = dot(sxv[...].astype(BF), gmat[way])
        row = dot(ysv[...].astype(BF), xmat[way])
        ab[way, :, : 2 * ny] = col
        ab[way, :, 2 * ny:] = row
        plane_out[way, 0] = ab[way, :shots]
        plane_out[way, 1] = ab[way, rhs - shots:]

    def averaged_terms(way):
        ext[:shots] = plane_in[way, 0]
        ext[shots:shots + rhs] = ab[way]
        ext[shots + rhs:rhs + 2 * shots] = plane_in[way, 1]
        near = ext[:rhs] + ext[2 * shots: 2 * shots + rhs]
        ab[way] = 0.5 * ext[shots:shots + rhs] + 0.25 * near

    def hop_copies(way):
        step = 1 - 2 * way
        col = pltpu.make_async_remote_copy(
            src_ref=c_out.at[way], dst_ref=c_in.at[way],
            send_sem=c_send.at[way], recv_sem=c_recv.at[way],
            device_id={"gx": gx + step}, device_id_type=MESH,
        )
        row = pltpu.make_async_remote_copy(
            src_ref=r_out.at[way], dst_ref=r_in.at[way],
            send_sem=r_send.at[way], recv_sem=r_recv.at[way],
            device_id={"gy": gy + step}, device_id_type=MESH,
        )
        return col, row

    def places(way):
        at_x = gx + way * (n_gx - 1 - 2 * gx)
        at_y = gy + way * (n_gy - 1 - 2 * gy)
        return at_x, at_y

    def hop(way):
        at_x, at_y = places(way)
        send_col, send_row = hop_copies(way)

        @pl.when(at_x > 0)
        def _():
            send_col.wait_recv()

        @pl.when(at_y > 0)
        def _():
            send_row.wait_recv()

        p = dot(c_in[way], gmat[way])
        q = dot(r_in[way], xmat[way])
        pq[way, :, : 2 * ny] = p
        pq[way, :, 2 * ny:] = q
        forward = jnp.broadcast_to(way == 0, (1, 1))

        def out_lane(value):
            n = value.shape[1]
            return jnp.where(forward, value[:, n - 1:], value[:, :1])

        ey, ex = edge[way, 0:1, : 2 * ny], edge[way, 0:1, 2 * ny:]
        eyr, eyi, exr, exi = ey[:, :ny], ey[:, ny:], ex[:, :nx], ex[:, nx:]
        pr, pi, qr, qi = p[:, :ny], p[:, ny:], q[:, :nx], q[:, nx:]
        xr, xi, yr, yi = out_lane(exr), out_lane(exi), out_lane(eyr), out_lane(eyi)
        tr, ti, sr, si = out_lane(pr), out_lane(pi), out_lane(qr), out_lane(qi)
        c_out[way, :, :ny] = (ab[way, :, :ny] + (pr * xr - pi * xi) + (eyr * sr - eyi * si)).astype(BF)
        c_out[way, :, ny:] = (
            ab[way, :, ny: 2 * ny] + (pr * xi + pi * xr) + (eyr * si + eyi * sr)
        ).astype(BF)

        @pl.when(at_x < n_gx - 1)
        def _():
            send_col.start()

        r_out[way, :, :nx] = (
            ab[way, :, 2 * ny: 2 * ny + nx] + (exr * tr - exi * ti) + (qr * yr - qi * yi)
        ).astype(BF)
        r_out[way, :, nx:] = (
            ab[way, :, 2 * ny + nx:] + (exr * ti + exi * tr) + (qr * yi + qi * yr)
        ).astype(BF)

        @pl.when(at_y < n_gy - 1)
        def _():
            send_row.start()

    def hop_departures(way):
        at_x, at_y = places(way)
        send_col, send_row = hop_copies(way)

        @pl.when(at_x < n_gx - 1)
        def _():
            send_col.wait_send()

        @pl.when(at_y < n_gy - 1)
        def _():
            send_row.wait_send()

    def base_fields(way):
        def two_depths(i, carry):
            s, d = i // (depths // 2), (i % (depths // 2)) * 2
            planes = []
            for part in range(2):
                low = src[way, s, part, pl.ds(d, 2)].astype(F32)
                mid = src[way, s, part, pl.ds(d + 1, 2)].astype(F32)
                high = src[way, s, part, pl.ds(d + 2, 2)].astype(F32)
                mean = 0.5 * mid + 0.25 * (low + high)
                planes.append(mean.astype(BF).reshape(2 * ny, nx))
            out = dot(jnp.concatenate(planes, axis=1), xmat[way])
            for k in range(2):
                half[k, :ny] = out[k * ny:(k + 1) * ny, :nx].astype(BF)
                half[k, ny:] = out[k * ny:(k + 1) * ny, nx:].astype(BF)
            for k in range(2):
                base[way, (d + k) * shots + s] = dot(ymat[way], half[k])
            return carry

        lax.fori_loop(0, shots * depths // 2, two_depths, 0)

    state_front = gx + gy
    last_front = n_gx + n_gy - 2
    first = jnp.where(2 * state_front <= last_front, 0, 1)
    second = 1 - first
    early = jnp.minimum(state_front, last_front - state_front)

    local_terms(first)
    pl.semaphore_wait(
        barrier,
        sum(
            (index > 0).astype(jnp.int32) + (index < count - 1).astype(jnp.int32)
            for index, count in ((gx, n_gx), (gy, n_gy), (gz, n_gz))
        ),
    )
    start_both(plane_copies(first))
    local_terms(second)
    start_both(plane_copies(second))
    start_both(halo_copies(first))
    start_both(halo_copies(second))
    wait_arrivals(plane_copies(first))
    averaged_terms(first)
    hop(first)
    wait_arrivals(plane_copies(second))
    averaged_terms(second)

    near_middle = early >= 3

    @pl.when(near_middle)
    def _():
        hop(second)

    wait_arrivals(halo_copies(first))
    base_fields(first)
    wait_arrivals(halo_copies(second))
    base_fields(second)

    @pl.when(jnp.logical_not(near_middle))
    def _():
        hop(second)

    for way in range(2):
        wait_departures(plane_copies(way))
        wait_departures(halo_copies(way))
        hop_departures(way)


def last_kernel(shots, ny, nx, base, pq, edge, state_out, adjoint_out, gradient):
    d = pl.program_id(0)
    rows = lax.broadcasted_iota(jnp.int32, (8, 1), 0)

    def stacked(first, second, third, fourth):
        lower = jnp.where(rows == 2, third, jnp.where(rows == 3, fourth, 0.0))
        return jnp.where(rows == 0, first, jnp.where(rows == 1, second, lower)).astype(BF)

    for way, out in ((0, state_out), (1, adjoint_out)):
        ey, ex = edge[way, 0:1, : 2 * ny], edge[way, 0:1, 2 * ny:]
        ey_turned = jnp.concatenate([-ey[:, ny:], ey[:, :ny]], axis=1)
        for s in range(shots):
            now = pq[way, pl.ds(d * shots + s, 1), :]
            p, q = now[:, : 2 * ny], now[:, 2 * ny:]
            turned = jnp.concatenate([-p[:, ny:], p[:, :ny]], axis=1)
            left = stacked(p, turned, ey, ey_turned)
            right = stacked(ex[:, :nx], ex[:, nx:], q[:, :nx], q[:, nx:])
            total = (base[way, d * shots + s] + dot_first(left, right)).astype(BF)
            out[s, 0, 0] = total[:ny]
            out[s, 1, 0] = total[ny:]
    acc = jnp.zeros((ny, nx), F32)
    for s in range(shots):
        acc = acc + state_out[s, 0, 0].astype(F32) * adjoint_out[s, 0, 0].astype(F32)
        acc = acc - state_out[s, 1, 0].astype(F32) * adjoint_out[s, 1, 0].astype(F32)
    gradient[0] = acc / shots


def per_device(source_field, adjoint_source, x_inverse, y_inverse):
    shots, _, depths, ny, nx = source_field.shape
    sizes = tuple(lax.axis_size(axis) for axis in ("gx", "gy", "gz"))
    rhs = shots * depths
    wide = 2 * (ny + nx)
    vmem = pltpu.VMEM
    dma = pltpu.SemaphoreType.DMA
    anywhere = pl.BlockSpec(memory_space=pltpu.HBM)
    operands = [
        pltpu.with_memory_space_constraint(value, pltpu.HBM)
        for value in (source_field, adjoint_source, x_inverse, y_inverse)
    ]
    base, pq, edge = pl.pallas_call(
        functools.partial(kernel, sizes, shots, depths, ny, nx),
        out_shape=(
            jax.ShapeDtypeStruct((2, rhs, 2 * ny, nx), F32),
            jax.ShapeDtypeStruct((2, rhs, wide), F32),
            jax.ShapeDtypeStruct((2, 8, wide), F32),
        ),
        in_specs=[anywhere] * 4,
        out_specs=(pl.BlockSpec(memory_space=vmem),) * 3,
        scratch_shapes=[
            vmem((2, shots, 2, depths + 2, ny, nx), BF),
            vmem((2, nx, nx), BF),
            vmem((2, ny, ny), BF),
            vmem((2, 2 * nx, 2 * nx), BF),
            vmem((2, 2 * ny, 2 * ny), BF),
            vmem((2, 2 * ny, 2 * ny), BF),
            vmem((rhs, 2 * ny), F32),
            vmem((rhs, 2 * nx), F32),
            vmem((rhs + 2 * shots, wide), F32),
            vmem((2, rhs, wide), F32),
            vmem((2, 2, shots, wide), F32),
            vmem((2, 2, shots, wide), F32),
            vmem((2, rhs, 2 * ny), BF),
            vmem((2, rhs, 2 * nx), BF),
            vmem((2, rhs, 2 * ny), BF),
            vmem((2, rhs, 2 * nx), BF),
            vmem((2, 2 * ny, nx), BF),
            dma((4,)),
            dma((2, 2)),
            dma((2, 2)),
            dma((2, 2)),
            dma((2, 2)),
            dma((2,)),
            dma((2,)),
            dma((2,)),
            dma((2,)),
        ],
        compiler_params=pltpu.CompilerParams(
            collective_id=0, has_side_effects=True, vmem_limit_bytes=LIMIT
        ),
    )(*operands)
    plane = pl.BlockSpec((shots, 2, 1, ny, nx), lambda d: (0, 0, d, 0, 0))
    return pl.pallas_call(
        functools.partial(last_kernel, shots, ny, nx),
        grid=(depths,),
        out_shape=(
            jax.ShapeDtypeStruct(source_field.shape, BF),
            jax.ShapeDtypeStruct(source_field.shape, BF),
            jax.ShapeDtypeStruct((depths, ny, nx), F32),
        ),
        in_specs=[pl.BlockSpec(memory_space=vmem)] * 3,
        out_specs=(plane, plane, pl.BlockSpec((1, ny, nx), lambda d: (d, 0, 0))),
        compiler_params=pltpu.CompilerParams(vmem_limit_bytes=LIMIT),
    )(base, pq, edge)


def solution(mesh):
    in_specs = (
        P(None, None, "gz", "gy", "gx"),
        P(None, None, "gz", "gy", "gx"),
        P("gx", "gy", None, None, None),
        P("gx", "gy", None, None, None),
    )
    out_specs = (
        P(None, None, "gz", "gy", "gx"),
        P(None, None, "gz", "gy", "gx"),
        P("gz", "gy", "gx"),
    )
    return jax.shard_map(
        per_device, mesh=mesh, in_specs=in_specs, out_specs=out_specs, check_vma=False
    )
```
